1024 devices in a mesh: pipe: 4 (over x), tensor: 32 (over z), dp: 8 (over y, core).
Axes of the slice: x: 4, y: 4, z: 32, core: 2. Of those that a mesh axis runs over, the one named last changes fastest.
Arguments:
- section_layers: int32 [4], replicated, may hold values from 9 to 11
- grad_out: bfloat16 [4, 8, 192, 4096], P('pipe', 'dp', 'tensor'), may hold values from -6 to 6
- gate_act: bfloat16 [4, 8, 192, 28672], P('pipe', 'dp', None, 'tensor'), may hold values from -6 to 6
- up_act: bfloat16 [4, 8, 192, 28672], P('pipe', 'dp', None, 'tensor'), may hold values from -6 to 6
- down_weight: bfloat16 [4, 28672, 4096], P('pipe', 'tensor'), may hold values from -0.09375 to 0.09375
Outputs:
- grad_gate: bfloat16 [4, 8, 192, 28672], P('pipe', 'dp', None, 'tensor')
- grad_up: bfloat16 [4, 8, 192, 28672], P('pipe', 'dp', None, 'tensor')
- grad_down_w: bfloat16 [4, 28672, 4096], P('pipe', ('tensor', 'dp'))
The draws below stay inside these ranges and needn't reach their ends.
All inputs are finite; a program needn't handle non-finite values.
Results may differ from the reference program's by a relative error of at most 0.013.
Values may be sent and summed in bfloat16 or wider, within the bound.
A program may use at most 64 MiB of HBM per device.

```python
import jax
import jax.numpy as jnp
from jax import lax

D_WIN = 4096
FF = 28672
ROWS = 192
SECTIONS = 4
REPLICAS = 8


def draw_section_layers(key, part):
    fresh = jax.random.fold_in(jax.random.fold_in(key, 731), 4099)
    key_counts, key_high, key_step = jax.random.split(fresh, 3)
    counts = jax.random.randint(key_counts, (SECTIONS,), 9, 12).astype(jnp.int32)
    high_section = jax.random.randint(key_high, (), 0, SECTIONS).astype(jnp.int32)
    step_over = jax.random.randint(key_step, (), 1, SECTIONS).astype(jnp.int32)
    low_section = ((high_section + step_over) % SECTIONS).astype(jnp.int32)
    positions = jnp.arange(SECTIONS, dtype=jnp.int32)
    counts = jnp.where(positions == high_section, jnp.int32(11), counts)
    counts = jnp.where(positions == low_section, jnp.int32(9), counts)
    return counts.astype(jnp.int32)


def spiked(values, key, source, target, shards_of, factor):
    owner, partner = [(jnp.arange(values.shape[axis_at]) // (values.shape[axis_at] // shards_of)).reshape([-1 if axis == axis_at else 1 for axis in range(values.ndim)]) for axis_at in (source, target)]
    chosen = jax.random.permutation(key, shards_of)[partner]
    strong = (owner == chosen) | (owner == (partner + shards_of // 2) % shards_of)
    return jnp.where(strong, factor * values, values)


def level_of(own_key, shape, pieces, least, top_value):
    level, own = 1.0, jax.random.fold_in(own_key, 6)
    for dim, blocks in pieces:
        steps = jnp.exp(jax.random.uniform(jax.random.fold_in(own, dim), (blocks,), jnp.float32, least / len(pieces), top_value / len(pieces)))
        level = level * jnp.repeat(steps, shape[dim] // blocks).reshape([-1 if axis == dim else 1 for axis in range(len(shape))])
    return level


def normal_values(key, extent, width, bound, cuts=(), held_as=jnp.bfloat16):
    loudness = level_of(key, extent, cuts, -0.22, 0.18) if cuts else 1.0
    drawn = jax.random.normal(key, extent, jnp.float32) * width * loudness
    return jnp.minimum(jnp.maximum(drawn, -bound), bound).astype(held_as)


def heavy_noise(own_key, extent, spread, bound, shards, heavy, kind=jnp.bfloat16):
    array = spread * jax.random.normal(own_key, extent, jnp.float32)
    if shards:
        array = array * level_of(own_key, extent, shards, -0.22, 0.18)
    return jnp.clip(spiked(array, jax.random.fold_in(own_key, 3), *heavy), -bound, bound).astype(kind)


def setup_inputs(seed: int = 0) -> dict:
    key_of = jax.random.split(jax.random.key(seed), 6)
    section_layers = draw_section_layers(jax.random.fold_in(key_of[5], 71), 0)
    grad_out = normal_values(key_of[1], (SECTIONS, REPLICAS, ROWS, D_WIN), 1.0, 6.0, ((0, 4), (1, 8), (2, 32)))
    gate_act = normal_values(key_of[2], (SECTIONS, REPLICAS, ROWS, FF), 1.0, 6.0, ((0, 4), (1, 8), (3, 32)))
    up_act = heavy_noise(key_of[3], (SECTIONS, REPLICAS, ROWS, FF), 1.0, 6.0, ((0, 4), (1, 8), (3, 32)), (1, 3, 8, 2.0))
    down_weight = normal_values(key_of[4], (SECTIONS, FF, D_WIN), D_WIN ** -0.5, 0.09375, ((0, 4), (1, 32)))
    return {"section_layers": section_layers, "grad_out": grad_out, "gate_act": gate_act, "up_act": up_act, "down_weight": down_weight}


def one_section(inputs):
    scale, grad_rows, gate_in, up_in, weight = inputs
    gate = gate_in.astype(jnp.float32)
    up = up_in.astype(jnp.float32)
    logistic = jax.nn.sigmoid(gate)
    activated = gate * logistic
    hidden = (activated * up).astype(jnp.bfloat16)
    norm_scale = scale / jnp.sqrt(jnp.float32(ROWS * REPLICAS))

    def per_replica(running, items):
        rows_here, hidden_here = items
        grad_hidden = scale * lax.dot_general(rows_here, weight, (((1,), (1,)), ((), ())), preferred_element_type=jnp.float32)
        partial_sum = norm_scale * lax.dot_general(hidden_here, rows_here, (((0,), (0,)), ((), ())), preferred_element_type=jnp.float32)
        partial_sum = lax.optimization_barrier(partial_sum.astype(jnp.bfloat16))
        return (running + partial_sum.astype(jnp.float32), grad_hidden)
    start_sum = jnp.zeros((FF, D_WIN), jnp.float32)
    summed, grad_hidden = lax.scan(per_replica, start_sum, (grad_rows, hidden))
    grad_gate = (grad_hidden * up * logistic * (1.0 + gate * (1.0 - logistic))).astype(jnp.bfloat16)
    grad_up = (grad_hidden * activated).astype(jnp.bfloat16)
    return (grad_gate, grad_up, summed.astype(jnp.bfloat16))

def reference(section_layers, grad_out, gate_act, up_act, down_weight):
    offset = (jnp.cumsum(section_layers) - section_layers).astype(jnp.int32)
    scale = jnp.sqrt(10.0 / (offset + section_layers).astype(jnp.float32))
    grad_gate, grad_up, grad_down_w = lax.map(one_section, (scale, grad_out, gate_act, up_act, down_weight))
    return (grad_gate, grad_up, grad_down_w)
```

```python
import functools

import jax
import jax.numpy as jnp
from jax import lax
from jax.experimental import pallas as pl
from jax.experimental.pallas import tpu as pltpu
from jax.sharding import PartitionSpec as P

MESH = pl.DeviceIdType.MESH
F32 = jnp.float32
BF16 = jnp.bfloat16
SPLITS = 2


def mm(a, b):
    return jnp.dot(a, b, preferred_element_type=F32)


def kernel(
    nz, npipe,
    layers_ref, go_hbm, gate_hbm, up_hbm, w_hbm,
    gg_ref, gu_ref, dw_ref,
    go, gate, up, w, pad, first, stage, mine, other, act, gfac,
    hidden_t, h_in, l_buf, sel_g, g_send, g_buf, d_send,
    load_sem, first_send, first_recv, zs, zr, ys, yr, hs, hr, ps, pr,
):
    rows, d = go.shape
    tokens, ff = gate.shape
    half, quarter = d // 2, d // 4
    fb = dw_ref.shape[1]
    f2 = 2 * fb
    ksize = 16 * nz
    width = quarter // SPLITS

    section = lax.axis_index("pipe")
    me = lax.axis_index("tensor")
    dp = lax.axis_index("dp")
    y, c = dp // 2, dp % 2

    def loads():
        return [
            pltpu.make_async_copy(go_hbm.at[0, 0], go, load_sem.at[0]),
            pltpu.make_async_copy(gate_hbm.at[0, 0], gate, load_sem.at[1]),
            pltpu.make_async_copy(up_hbm.at[0, 0], up, load_sem.at[2]),
            pltpu.make_async_copy(w_hbm.at[0], w, load_sem.at[3]),
        ]

    load_go, load_gate, load_up, load_w = loads()
    for one in (load_go, load_gate, load_up, load_w):
        one.start()

    right = lax.rem(me + 1, nz)
    left = lax.rem(me + nz - 1, nz)
    barrier = pltpu.get_barrier_semaphore()
    for k in range(1, 8):
        pl.semaphore_signal(barrier, inc=1, device_id={"dp": lax.rem(dp + k, 8)}, device_id_type=MESH)
    for z in (left, right):
        pl.semaphore_signal(barrier, inc=1, device_id={"tensor": z}, device_id_type=MESH)

    def place(core):
        even = 1 - lax.rem(y + 4 - core, 2)
        mate = lax.rem(y + 4 + 2 * even - 1, 4)
        outer = lax.rem(y + 4 - 2 * even + 1, 4)
        return 1 - even, mate, outer

    m_own, mate_own, outer_own = place(c)
    m_par, mate_par, _ = place(1 - c)
    q_own = 2 * m_own + c
    base_own = lax.rem(y + 4 - m_own, 4)
    partner = 2 * y + 1 - c

    load_go.wait()
    pad[...] = jnp.zeros_like(pad)
    for h in range(2):
        for u in range(2):
            at = h * half + u * quarter
            pad[h, 8 * u:8 * u + rows, :] = go[:, at:at + quarter].astype(F32)
    first[...] = pad[...].astype(BF16)

    pl.semaphore_wait(barrier, 9)

    def first_copy(target_dp, h, q, k):
        return pltpu.make_async_remote_copy(
            src_ref=first.at[h], dst_ref=stage.at[q], send_sem=first_send.at[k], recv_sem=first_recv.at[q],
            device_id={"dp": target_dp}, device_id_type=MESH,
        )

    firsts = [
        first_copy(2 * mate_own + c, c, q_own, 0),
        first_copy(2 * mate_par + 1 - c, 1 - c, 2 * m_par + c, 1),
        first_copy(partner, 1 - c, 2 * m_par + c, 2),
    ]
    for one in firsts:
        one.start()
    stage[q_own] = first[c]

    load_gate.wait()
    load_up.wait()
    g32 = gate[...].astype(F32)
    u32 = up[...].astype(F32)
    logistic = 1.0 / (1.0 + jnp.exp(-g32))
    activated = g32 * logistic
    act[...] = activated
    gfac[...] = u32 * logistic * (1.0 + g32 * (1.0 - logistic))
    hidden_t[...] = jnp.transpose((activated * u32).astype(BF16).astype(F32)).astype(BF16)

    def h_copy(k, slot):
        to = lax.rem(y + k, 4)
        return pltpu.make_async_remote_copy(
            src_ref=hidden_t.at[pl.ds(pl.multiple_of(to * f2, 16), f2), :], dst_ref=h_in.at[c, slot],
            send_sem=hs.at[k], recv_sem=hr.at[slot],
            device_id={"dp": 2 * to + c}, device_id_type=MESH,
        )

    for k in (1, 2, 3):
        h_copy(k, y).start()
    h_in[c, y] = hidden_t[pl.ds(pl.multiple_of(y * f2, 16), f2), :]

    for k in (1, 2, 3):
        first_copy(partner, 0, lax.rem(q_own + k, 4), 0).wait_recv()

    r = lax.broadcasted_iota(jnp.int32, (48, 64), 0)
    k = lax.broadcasted_iota(jnp.int32, (48, 64), 1)
    low = r % 16
    rho = jnp.where(r < 32, low, 16 + low % 8)
    u_of = jnp.where(r < 32, r // 16, low // 8)
    source = (rho // rows) * 16 + 8 * u_of + rho % rows
    pick = (source == k).astype(F32).astype(BF16)
    built = mm(pick, stage[...].reshape(64, quarter)).astype(BF16)
    for j in range(3):
        mine[j, 0:16, :] = built[16 * j:16 * j + 16, :]

    def z_copy(direction, slot, later, j, s, step):
        return pltpu.make_async_remote_copy(
            src_ref=mine.at[j, pl.ds(pl.multiple_of(16 * slot, 16), 16), pl.ds(s * width, width)],
            dst_ref=mine.at[j, pl.ds(pl.multiple_of(16 * later, 16), 16), pl.ds(s * width, width)],
            send_sem=zs.at[direction, lax.rem(step, 2), j, s], recv_sem=zr.at[direction, step, j, s],
            device_id={"tensor": right if direction == 0 else left}, device_id_type=MESH,
        )

    def y_copy(direction, slot, step):
        at = pl.ds(pl.multiple_of(16 * slot, 16), 16)
        return pltpu.make_async_remote_copy(
            src_ref=mine.at[:, at, :], dst_ref=other.at[:, at, :],
            send_sem=ys.at[direction, lax.rem(step, 2)], recv_sem=yr.at[slot],
            device_id={"dp": 2 * outer_own + c}, device_id_type=MESH,
        )

    blocks = [(j, s) for j in range(3) for s in range(SPLITS)]
    for j, s in blocks:
        z_copy(0, 0, 1, j, s, 0).start()
        z_copy(1, 0, nz - 1, j, s, 0).start()
    y_copy(0, 0, 0).start()

    top = nz // 2

    def step(d, carry):
        for j, s in blocks:
            z_copy(0, d - 1, d, j, s, d - 1).wait_recv()
            z_copy(0, d - 1, d, j, s, d - 1).wait_send()
            z_copy(0, d, d + 1, j, s, d).start()
            z_copy(1, nz - d, nz - d, j, s, d - 1).wait_recv()
            z_copy(1, nz - d, nz - d, j, s, d - 1).wait_send()

            @pl.when(d < top - 1)
            def _():
                z_copy(1, nz - d, nz - d - 1, j, s, d).start()

        @pl.when(d >= 2)
        def _():
            y_copy(0, d, d).wait_send()

        @pl.when(d >= 3)
        def _():
            y_copy(1, d, d).wait_send()

        y_copy(0, d, d).start()
        y_copy(1, nz - d, d).start()
        return carry

    def run(start, stop):
        lax.fori_loop(start, stop, step, 0)

    run(1, min(3, top))

    for k in (1, 2, 3):
        h_copy(1, lax.rem(y + k, 4)).wait_recv()
    h_pass = pltpu.make_async_remote_copy(
        src_ref=h_in.at[c], dst_ref=h_in.at[c], send_sem=ps.at[0], recv_sem=pr.at[0],
        device_id={"dp": partner}, device_id_type=MESH,
    )
    h_pass.start()
    run(3, min(6, top))

    t = lax.broadcasted_iota(jnp.int32, (tokens, ksize), 0)
    col = lax.broadcasted_iota(jnp.int32, (tokens, ksize), 1)
    z_rows = lax.rem(me + nz - col // 16, nz) * rows
    low = col % 16

    def select(q, kind):
        if kind == 0:
            rho, valid = low, low >= 0
        else:
            rho, valid = 16 + low % 8, (low // 8) == (kind - 1)
        i = rho - rows * q
        hit = valid & (i >= 0) & (i < rows) & (t == z_rows + i)
        return jnp.where(hit, 1.0, 0.0).astype(BF16)

    for kind in range(3):
        for cc in range(2):
            sel_g[kind, cc * tokens:(cc + 1) * tokens, :] = select(2 * m_own + cc, kind)
    run(6, min(8, top))
    h_pass.wait_recv()
    for group in range(2):
        base = lax.rem(base_own + 2 * group, 4)
        for kind in range(3):
            total = None
            for q in ((0, 1, 2) if kind == 0 else (2, 3)):
                h_q = h_in[q % 2, lax.rem(base + q // 2, 4)]
                term = mm(h_q, select(q, kind))
                total = term if total is None else total + term
            l_buf[group, kind] = total.astype(BF16)
    run(8, top)

    for j, s in blocks:
        z_copy(0, top - 1, top, j, s, top - 1).wait_recv()
        z_copy(0, top - 1, top, j, s, top - 1).wait_send()
    y_copy(0, top, top).wait_send()
    y_copy(0, top, top).start()

    tile = 256 if quarter % 256 == 0 else 128
    tiles = quarter // tile
    here = pl.multiple_of(c * half, half)

    for u in range(2):
        @pl.loop(0, tiles)
        def _(n):
            at = pl.ds(pl.multiple_of(n * tile, tile), tile)
            got = mm(sel_g[0], mine[u, :, at]) + mm(sel_g[1 + u], mine[2, :, at])
            both = got.astype(BF16)
            top_rows, bottom_rows = both[:tokens], both[tokens:]
            own_rows = jnp.where(c == 0, top_rows.astype(F32), bottom_rows.astype(F32)).astype(BF16)
            par_rows = jnp.where(c == 0, bottom_rows.astype(F32), top_rows.astype(F32)).astype(BF16)
            g_buf[:, pl.ds(pl.multiple_of(here + u * quarter + n * tile, tile), tile)] = own_rows
            g_send[:, pl.ds(pl.multiple_of(u * quarter + n * tile, tile), tile)] = par_rows

    g_pass = pltpu.make_async_remote_copy(
        src_ref=g_send, dst_ref=g_buf.at[:, pl.ds(here, half)], send_sem=ps.at[1], recv_sem=pr.at[1],
        device_id={"dp": partner}, device_id_type=MESH,
    )
    g_pass.start()

    before = jnp.int32(0)
    for k in range(npipe):
        before = before + jnp.where(section >= k, layers_ref[k], 0)
    scale = jnp.sqrt(10.0 / jnp.full((1, 128), before, jnp.int32).astype(F32))[:, :1]
    norm_scale = scale / jnp.sqrt(jnp.full((1, 1), tokens * 8, F32))

    for slot in range(nz):
        y_copy(0, slot, 0).wait_recv()

    for u in range(2):
        @pl.loop(0, tiles)
        def _(n):
            at = pl.ds(pl.multiple_of(n * tile, tile), tile)
            total = mm(l_buf[0, 0], mine[u, :, at]) + mm(l_buf[0, 1 + u], mine[2, :, at])
            total = total + mm(l_buf[1, 0], other[u, :, at]) + mm(l_buf[1, 1 + u], other[2, :, at])
            total = total * norm_scale
            low_rows, high_rows = total[:fb], total[fb:]
            dw_ref[0, :, pl.ds(pl.multiple_of(here + u * quarter + n * tile, tile), tile)] = jnp.where(
                c == 0, low_rows, high_rows).astype(BF16)
            d_send[:, pl.ds(pl.multiple_of(u * quarter + n * tile, tile), tile)] = jnp.where(
                c == 0, high_rows, low_rows).astype(BF16)

    d_pass = pltpu.make_async_remote_copy(
        src_ref=d_send, dst_ref=dw_ref.at[0, :, pl.ds(here, half)], send_sem=ps.at[2], recv_sem=pr.at[2],
        device_id={"dp": partner}, device_id_type=MESH,
    )
    d_pass.start()

    load_w.wait()
    g_pass.wait_recv()
    at = 0
    while at < ff:
        n = min(256, ff - at)
        gh = scale * lax.dot_general(
            g_buf[...], w[at:at + n, :], (((1,), (1,)), ((), ())), preferred_element_type=F32)
        gg_ref[0, 0, :, at:at + n] = (gh * gfac[:, at:at + n]).astype(BF16)
        gu_ref[0, 0, :, at:at + n] = (gh * act[:, at:at + n]).astype(BF16)
        at += n

    y_copy(0, top, top).wait_send()
    y_copy(0, top, top - 1).wait_send()
    y_copy(1, top, top - 1).wait_send()
    if top > 2:
        y_copy(1, top, top - 2).wait_send()
    for one in firsts:
        one.wait_send()
    for k in (1, 2, 3):
        h_copy(k, y).wait_send()
    h_pass.wait_send()
    g_pass.wait_send()
    d_pass.wait()


def per_device(section_layers, grad_out, gate_act, up_act, down_weight, *, sizes):
    npipe, nz = sizes
    rows, d = grad_out.shape[2:]
    tokens, ff = gate_act.shape[2:]
    fb = ff // 8
    ksize = 16 * nz
    any_spec = pl.BlockSpec(memory_space=pl.ANY)
    vmem_spec = pl.BlockSpec(memory_space=pltpu.VMEM)
    return pl.pallas_call(
        functools.partial(kernel, nz, npipe),
        out_shape=(
            jax.ShapeDtypeStruct(gate_act.shape, BF16),
            jax.ShapeDtypeStruct(gate_act.shape, BF16),
            jax.ShapeDtypeStruct((1, fb, d), BF16),
        ),
        in_specs=[pl.BlockSpec(memory_space=pltpu.SMEM)] + [any_spec] * 4,
        out_specs=(vmem_spec,) * 3,
        scratch_shapes=[
            pltpu.VMEM((rows, d), BF16),
            pltpu.VMEM((tokens, ff), BF16),
            pltpu.VMEM((tokens, ff), BF16),
            pltpu.VMEM((ff, d), BF16),
            pltpu.VMEM((2, 16, d // 4), F32),
            pltpu.VMEM((2, 16, d // 4), BF16),
            pltpu.VMEM((4, 16, d // 4), BF16),
            pltpu.VMEM((3, ksize, d // 4), BF16),
            pltpu.VMEM((3, ksize, d // 4), BF16),
            pltpu.VMEM((tokens, ff), F32),
            pltpu.VMEM((tokens, ff), F32),
            pltpu.VMEM((ff, tokens), BF16),
            pltpu.VMEM((2, 4, 2 * fb, tokens), BF16),
            pltpu.VMEM((2, 3, 2 * fb, ksize), BF16),
            pltpu.VMEM((3, 2 * tokens, ksize), BF16),
            pltpu.VMEM((tokens, d // 2), BF16),
            pltpu.VMEM((tokens, d), BF16),
            pltpu.VMEM((fb, d // 2), BF16),
            pltpu.SemaphoreType.DMA((4,)),
            pltpu.SemaphoreType.DMA((3,)),
            pltpu.SemaphoreType.DMA((4,)),
            pltpu.SemaphoreType.DMA((2, 2, 3, SPLITS)),
            pltpu.SemaphoreType.DMA((2, nz // 2, 3, SPLITS)),
            pltpu.SemaphoreType.DMA((2, 2)),
            pltpu.SemaphoreType.DMA((nz,)),
            pltpu.SemaphoreType.DMA((4,)),
            pltpu.SemaphoreType.DMA((4,)),
            pltpu.SemaphoreType.DMA((3,)),
            pltpu.SemaphoreType.DMA((3,)),
        ],
        compiler_params=pltpu.CompilerParams(
            collective_id=0, has_side_effects=True, vmem_limit_bytes=60 * 2**20
        ),
    )(section_layers, grad_out, gate_act, up_act, down_weight)


def solution(mesh):
    placed = (
        P(),
        P("pipe", "dp", "tensor", None),
        P("pipe", "dp", None, "tensor"),
        P("pipe", "dp", None, "tensor"),
        P("pipe", "tensor", None),
    )
    return jax.shard_map(
        functools.partial(per_device, sizes=(mesh.shape["pipe"], mesh.shape["tensor"])),
        mesh=mesh,
        in_specs=placed,
        out_specs=(
            P("pipe", "dp", None, "tensor"),
            P("pipe", "dp", None, "tensor"),
            P("pipe", ("tensor", "dp"), None),
        ),
        check_vma=False,
    )
```

```python
import functools

import jax
import jax.numpy as jnp
from jax import lax
from jax.experimental import pallas as pl
from jax.experimental.pallas import tpu as pltpu
from jax.sharding import PartitionSpec as P

MESH = pl.DeviceIdType.MESH
F32 = jnp.float32
BF16 = jnp.bfloat16
SPLITS = 4


def mm(a, b):
    return jnp.dot(a, b, preferred_element_type=F32)


def kernel(
    nz, npipe,
    layers_ref, go_hbm, gate_hbm, up_hbm, w_hbm,
    gg_ref, gu_ref, dw_ref,
    go, gate, up, w, pad, first, stage, mine, other, act, gfac,
    hidden_t, h_in, l_buf, sel_g, g_send, g_recv, g_buf, d_send, d_recv, d_own,
    load_sem, first_send, first_recv, zs, zr, ys, yr, hs, hr, ps, pr,
):
    rows, d_model = go.shape
    tokens, ff = gate.shape
    half = d_model // 2
    fb = dw_ref.shape[1]
    f2 = 2 * fb
    top = nz // 2
    ksize = 16 * top
    part = rows * top
    width = half // SPLITS

    section = lax.axis_index("pipe")
    me = lax.axis_index("tensor")
    dp = lax.axis_index("dp")
    y, c = dp // 2, dp % 2

    load_go = pltpu.make_async_copy(go_hbm.at[0, 0], go, load_sem.at[0])
    load_gate = pltpu.make_async_copy(gate_hbm.at[0, 0], gate, load_sem.at[1])
    load_up = pltpu.make_async_copy(up_hbm.at[0, 0], up, load_sem.at[2])
    load_w = pltpu.make_async_copy(w_hbm.at[0], w, load_sem.at[3])
    load_go.start()

    right = lax.rem(me + 1, nz)
    left = lax.rem(me + nz - 1, nz)
    ahead = jnp.where(c == 0, right, left)
    barrier = pltpu.get_barrier_semaphore()
    for k in range(1, 8):
        pl.semaphore_signal(barrier, inc=1, device_id={"dp": lax.rem(dp + k, 8)}, device_id_type=MESH)
    for z in (left, right):
        pl.semaphore_signal(barrier, inc=1, device_id={"tensor": z}, device_id_type=MESH)
    load_gate.start()
    load_up.start()

    def place(core):
        even = 1 - lax.rem(y + 4 - core, 2)
        mate = lax.rem(y + 4 + 2 * even - 1, 4)
        outer = lax.rem(y + 4 - 2 * even + 1, 4)
        return 1 - even, mate, outer

    m_own, mate_own, outer_own = place(c)
    m_par, mate_par, _ = place(1 - c)
    q_own = 2 * m_own + c
    q_par = 2 * m_own + 1 - c
    base_own = lax.rem(y + 4 - m_own, 4)
    partner = 2 * y + 1 - c

    pad[...] = jnp.zeros_like(pad)
    load_go.wait()
    for u in range(2):
        pad[8 * u:8 * u + rows, :] = go[:, u * half:(u + 1) * half].astype(F32)
    first[...] = pad[...].astype(BF16)

    pl.semaphore_wait(barrier, 9)

    def first_copy(target_dp, q, k):
        return pltpu.make_async_remote_copy(
            src_ref=first, dst_ref=stage.at[q], send_sem=first_send.at[k], recv_sem=first_recv.at[q],
            device_id={"dp": target_dp}, device_id_type=MESH,
        )

    firsts = [
        first_copy(2 * mate_own + c, q_own, 0),
        first_copy(2 * mate_par + 1 - c, 2 * m_par + c, 1),
        first_copy(partner, 2 * m_par + c, 2),
    ]
    for one in firsts:
        one.start()
    stage[q_own] = first[...]

    load_gate.wait()
    load_up.wait()
    g32 = gate[...].astype(F32)
    u32 = up[...].astype(F32)
    logistic = 1.0 / (1.0 + jnp.exp(-g32))
    activated = g32 * logistic
    act[...] = activated
    gfac[...] = u32 * logistic * (1.0 + g32 * (1.0 - logistic))

    for k in (1, 2, 3):
        first_copy(partner, lax.rem(q_own + k, 4), 0).wait_recv()

    def pos(d):
        return lax.rem(d + top + c, top + 1)

    def at_slot(d):
        return pl.ds(pl.multiple_of(16 * pos(d), 16), 16)

    r = lax.broadcasted_iota(jnp.int32, (48, 64), 0)
    k = lax.broadcasted_iota(jnp.int32, (48, 64), 1)
    low = r % 16
    rho = jnp.where(r < 32, low, 16 + low % 8)
    u_of = jnp.where(r < 32, r // 16, low // 8)
    source = (rho // rows) * 16 + 8 * u_of + rho % rows
    pick = (source == k).astype(F32).astype(BF16)
    built = mm(pick, stage[...].reshape(64, half)).astype(BF16)
    for j in range(3):
        mine[j, at_slot(0), :] = built[16 * j:16 * j + 16, :]

    def z_copy(d, j, s):
        cols = pl.ds(s * width, width)
        return pltpu.make_async_remote_copy(
            src_ref=mine.at[j, at_slot(d), cols], dst_ref=mine.at[j, at_slot(d + 1), cols],
            send_sem=zs.at[lax.rem(d, 2), j, s], recv_sem=zr.at[d, j, s],
            device_id={"tensor": ahead}, device_id_type=MESH,
        )

    def y_copy(d):
        return pltpu.make_async_remote_copy(
            src_ref=mine.at[:, at_slot(d), :], dst_ref=other.at[:, at_slot(d), :],
            send_sem=ys.at[lax.rem(d, 2)], recv_sem=yr.at[pos(d)],
            device_id={"dp": 2 * outer_own + c}, device_id_type=MESH,
        )

    blocks = [(j, s) for j in range(3) for s in range(SPLITS)]
    for j, s in blocks:
        z_copy(0, j, s).start()

    @pl.when(c == 1)
    def _():
        y_copy(0).start()

    load_w.start()

    hidden_t[...] = jnp.transpose((act[...] * up[...].astype(F32)).astype(BF16).astype(F32)).astype(BF16)

    def h_copy(k, slot):
        to = lax.rem(y + k, 4)
        return pltpu.make_async_remote_copy(
            src_ref=hidden_t.at[pl.ds(pl.multiple_of(to * f2, 16), f2), :], dst_ref=h_in.at[c, slot],
            send_sem=hs.at[k], recv_sem=hr.at[slot],
            device_id={"dp": 2 * to + c}, device_id_type=MESH,
        )

    for k in (1, 2, 3):
        h_copy(k, y).start()
    h_in[c, y] = hidden_t[pl.ds(pl.multiple_of(y * f2, 16), f2), :]

    def step(d, carry):
        for j, s in blocks:
            @pl.when(d >= 2)
            def _():
                z_copy(d, j, s).wait_send()

            z_copy(d - 1, j, s).wait_recv()

            @pl.when(d < top - c)
            def _():
                z_copy(d, j, s).start()

        @pl.when(d >= 3 - c)
        def _():
            y_copy(d).wait_send()

        y_copy(d).start()
        return carry

    def run(start, stop):
        lax.fori_loop(start, stop, step, 0)

    run(1, min(3, top))

    for k in (1, 2, 3):
        h_copy(1, lax.rem(y + k, 4)).wait_recv()
    h_pass = pltpu.make_async_remote_copy(
        src_ref=h_in.at[c], dst_ref=h_in.at[c], send_sem=ps.at[0], recv_sem=pr.at[0],
        device_id={"dp": partner}, device_id_type=MESH,
    )
    h_pass.start()
    run(3, min(6, top))

    def z_of(p, core):
        return lax.rem(jnp.where(core == 0, me + nz - 1 - p, me + p), nz)

    def select(count, q, kind, natural):
        t = lax.broadcasted_iota(jnp.int32, (count, ksize), 0)
        col = lax.broadcasted_iota(jnp.int32, (count, ksize), 1)
        low = col % 16
        p = col // 16
        start = (z_of(p, c) if natural else p) * rows
        if kind == 0:
            rho, valid = low, low >= 0
        else:
            rho, valid = 16 + low % 8, (low // 8) == (kind - 1)
        i = rho - rows * q
        hit = valid & (i >= 0) & (i < rows) & (t == start + i)
        return jnp.where(hit, 1.0, 0.0).astype(BF16)

    for kind in range(3):
        sel_g[kind, :tokens, :] = select(tokens, q_own, kind, True)
        sel_g[kind, tokens:, :] = select(part, q_par, kind, False)
    run(6, min(8, top))
    h_pass.wait_recv()
    for group in range(2):
        base = lax.rem(base_own + 2 * group, 4)
        for kind in range(3):
            total = None
            for q in ((0, 1, 2) if kind == 0 else (2, 3)):
                h_q = h_in[q % 2, lax.rem(base + q // 2, 4)]
                term = mm(h_q, select(tokens, q, kind, True))
                total = term if total is None else total + term
            l_buf[group, kind] = total.astype(BF16)
    run(8, top)

    @pl.when(c == 0)
    def _():
        for j, s in blocks:
            z_copy(top - 1, j, s).wait_recv()
        if top > 2:
            y_copy(top).wait_send()
        y_copy(top).start()

    tile = 256 if half % 256 == 0 else 128
    tiles = half // tile

    def tile_at(u, n):
        return pl.ds(pl.multiple_of(u * half + n * tile, tile), tile)

    for u in range(2):
        @pl.loop(0, tiles)
        def _(n):
            at = tile_at(0, n)
            got = mm(sel_g[0], mine[u, 0:ksize, at]) + mm(sel_g[1 + u], mine[2, 0:ksize, at])
            both = got.astype(BF16)
            g_buf[:, tile_at(u, n)] = both[:tokens]
            g_send[:, tile_at(u, n)] = both[tokens:]

    g_pass = pltpu.make_async_remote_copy(
        src_ref=g_send, dst_ref=g_recv, send_sem=ps.at[1], recv_sem=pr.at[1],
        device_id={"dp": partner}, device_id_type=MESH,
    )
    g_pass.start()

    before = jnp.int32(0)
    for k in range(npipe):
        before = before + jnp.where(section >= k, layers_ref[k], 0)
    scale = jnp.sqrt(10.0 / jnp.full((1, 128), before, jnp.int32).astype(F32))[:, :1]
    norm_scale = scale / jnp.sqrt(jnp.full((1, 1), tokens * 8, F32))

    for p in range(top):
        pltpu.make_async_remote_copy(
            src_ref=mine.at[:, 0:16, :], dst_ref=other.at[:, 16 * p:16 * p + 16, :],
            send_sem=ys.at[0], recv_sem=yr.at[p],
            device_id={"dp": 2 * outer_own + c}, device_id_type=MESH,
        ).wait_recv()

    for u in range(2):
        @pl.loop(0, tiles)
        def _(n):
            at = tile_at(0, n)
            total = mm(l_buf[0, 0], mine[u, 0:ksize, at]) + mm(l_buf[0, 1 + u], mine[2, 0:ksize, at])
            total = total + mm(l_buf[1, 0], other[u, 0:ksize, at]) + mm(l_buf[1, 1 + u], other[2, 0:ksize, at])
            total = total * norm_scale
            low_rows, high_rows = total[:fb], total[fb:]
            d_own[:, tile_at(u, n)] = jnp.where(c == 0, low_rows, high_rows)
            d_send[:, tile_at(u, n)] = jnp.where(c == 0, high_rows, low_rows).astype(BF16)

    d_pass = pltpu.make_async_remote_copy(
        src_ref=d_send, dst_ref=d_recv, send_sem=ps.at[2], recv_sem=pr.at[2],
        device_id={"dp": partner}, device_id_type=MESH,
    )
    d_pass.start()

    t = lax.broadcasted_iota(jnp.int32, (tokens, part), 0)
    col = lax.broadcasted_iota(jnp.int32, (tokens, part), 1)
    spread = jnp.where(t == z_of(col // rows, 1 - c) * rows + col % rows, 1.0, 0.0).astype(BF16)
    g_pass.wait_recv()

    @pl.loop(0, 2 * tiles)
    def _(n):
        at = tile_at(0, n)
        g_buf[:, at] = (g_buf[:, at].astype(F32) + mm(spread, g_recv[:, at])).astype(BF16)

    load_w.wait()
    at = 0
    while at < ff:
        n = min(256, ff - at)
        gh = scale * lax.dot_general(
            g_buf[...], w[at:at + n, :], (((1,), (1,)), ((), ())), preferred_element_type=F32)
        gg_ref[0, 0, :, at:at + n] = (gh * gfac[:, at:at + n]).astype(BF16)
        gu_ref[0, 0, :, at:at + n] = (gh * act[:, at:at + n]).astype(BF16)
        at += n

    d_pass.wait()

    @pl.loop(0, 2 * tiles)
    def _(n):
        at = tile_at(0, n)
        dw_ref[0, :, at] = (d_own[:, at] + d_recv[:, at].astype(F32)).astype(BF16)

    y_copy(0).wait_send()
    y_copy(1).wait_send()
    for j, s in blocks:
        z_copy(top, j, s).wait_send()

        @pl.when(c == 0)
        def _():
            z_copy(top - 1, j, s).wait_send()
    for one in firsts:
        one.wait_send()
    for k in (1, 2, 3):
        h_copy(k, y).wait_send()
    h_pass.wait_send()
    g_pass.wait_send()


def put_out(gg_ref, gu_ref, dw_ref, gg_hbm, gu_hbm, dw_hbm, sem):
    copies = [
        pltpu.make_async_copy(gg_ref, gg_hbm, sem.at[0]),
        pltpu.make_async_copy(gu_ref, gu_hbm, sem.at[1]),
        pltpu.make_async_copy(dw_ref, dw_hbm, sem.at[2]),
    ]
    for one in copies:
        one.start()
    for one in copies:
        one.wait()


def per_device(section_layers, grad_out, gate_act, up_act, down_weight, *, sizes):
    npipe, nz = sizes
    rows, d = grad_out.shape[2:]
    tokens, ff = gate_act.shape[2:]
    fb = ff // 8
    top = nz // 2
    ksize = 16 * top
    part = rows * top
    any_spec = pl.BlockSpec(memory_space=pltpu.HBM)
    vmem_spec = pl.BlockSpec(memory_space=pltpu.VMEM)
    outs = (
        jax.ShapeDtypeStruct(gate_act.shape, BF16),
        jax.ShapeDtypeStruct(gate_act.shape, BF16),
        jax.ShapeDtypeStruct((1, fb, d), BF16),
    )
    section_layers, grad_out, gate_act, up_act, down_weight = (
        pltpu.with_memory_space_constraint(x, pltpu.HBM) for x in (section_layers, grad_out, gate_act, up_act, down_weight))
    got = pl.pallas_call(
        functools.partial(kernel, nz, npipe),
        out_shape=outs,
        in_specs=[pl.BlockSpec(memory_space=pltpu.SMEM)] + [any_spec] * 4,
        out_specs=(vmem_spec,) * 3,
        scratch_shapes=[
            pltpu.VMEM((rows, d), BF16),
            pltpu.VMEM((tokens, ff), BF16),
            pltpu.VMEM((tokens, ff), BF16),
            pltpu.VMEM((ff, d), BF16),
            pltpu.VMEM((16, d // 2), F32),
            pltpu.VMEM((16, d // 2), BF16),
            pltpu.VMEM((4, 16, d // 2), BF16),
            pltpu.VMEM((3, ksize + 16, d // 2), BF16),
            pltpu.VMEM((3, ksize + 16, d // 2), BF16),
            pltpu.VMEM((tokens, ff), F32),
            pltpu.VMEM((tokens, ff), F32),
            pltpu.VMEM((ff, tokens), BF16),
            pltpu.VMEM((2, 4, 2 * fb, tokens), BF16),
            pltpu.VMEM((2, 3, 2 * fb, ksize), BF16),
            pltpu.VMEM((3, tokens + part, ksize), BF16),
            pltpu.VMEM((part, d), BF16),
            pltpu.VMEM((part, d), BF16),
            pltpu.VMEM((tokens, d), BF16),
            pltpu.VMEM((fb, d), BF16),
            pltpu.VMEM((fb, d), BF16),
            pltpu.VMEM((fb, d), F32),
            pltpu.SemaphoreType.DMA((4,)),
            pltpu.SemaphoreType.DMA((3,)),
            pltpu.SemaphoreType.DMA((4,)),
            pltpu.SemaphoreType.DMA((2, 3, SPLITS)),
            pltpu.SemaphoreType.DMA((top, 3, SPLITS)),
            pltpu.SemaphoreType.DMA((2,)),
            pltpu.SemaphoreType.DMA((top,)),
            pltpu.SemaphoreType.DMA((4,)),
            pltpu.SemaphoreType.DMA((4,)),
            pltpu.SemaphoreType.DMA((3,)),
            pltpu.SemaphoreType.DMA((3,)),
        ],
        compiler_params=pltpu.CompilerParams(
            collective_id=0, has_side_effects=True, vmem_limit_bytes=44 * 2**20
        ),
    )(section_layers, grad_out, gate_act, up_act, down_weight)
    return pl.pallas_call(
        put_out,
        out_shape=outs,
        in_specs=[vmem_spec] * 3,
        out_specs=(any_spec,) * 3,
        scratch_shapes=[pltpu.SemaphoreType.DMA((3,))],
        compiler_params=pltpu.CompilerParams(vmem_limit_bytes=8 * 2**20),
    )(*got)


def solution(mesh):
    placed = (
        P(),
        P("pipe", "dp", "tensor", None),
        P("pipe", "dp", None, "tensor"),
        P("pipe", "dp", None, "tensor"),
        P("pipe", "tensor", None),
    )
    return jax.shard_map(
        functools.partial(per_device, sizes=(mesh.shape["pipe"], mesh.shape["tensor"])),
        mesh=mesh,
        in_specs=placed,
        out_specs=(
            P("pipe", "dp", None, "tensor"),
            P("pipe", "dp", None, "tensor"),
            P("pipe", ("tensor", "dp"), None),
        ),
        check_vma=False,
    )
```

```python
import functools

import jax
import jax.numpy as jnp
from jax import lax
from jax.experimental import pallas as pl
from jax.experimental.pallas import tpu as pltpu
from jax.sharding import PartitionSpec as P

MESH = pl.DeviceIdType.MESH
F32 = jnp.float32
BF16 = jnp.bfloat16
SPLITS = 4


def mm(a, b):
    return jnp.dot(a, b, preferred_element_type=F32)


def kernel(
    nz, npipe,
    layers_ref, go_hbm, gate_hbm, up_hbm, w_hbm,
    gg_ref, gu_ref, dw_ref,
    go, gate, up, w, pad, first, stage, mine, other, act, gfac,
    hidden_t, h_in, l_buf, sel_g, g_send, g_recv, g_buf, d_send, d_recv, d_own,
    load_sem, first_send, first_recv, zs, zr, ys, yr, hs, hr, ps, pr,
):
    rows, d_model = go.shape
    tokens, ff = gate.shape
    half = d_model // 2
    fb = dw_ref.shape[1]
    f2 = 2 * fb
    top = nz // 2
    ksize = 16 * top
    part = rows * top
    width = half // SPLITS

    section = lax.axis_index("pipe")
    me = lax.axis_index("tensor")
    dp = lax.axis_index("dp")
    y, c = dp // 2, dp % 2

    load_go = pltpu.make_async_copy(go_hbm.at[0, 0], go, load_sem.at[0])
    load_gate = pltpu.make_async_copy(gate_hbm.at[0, 0], gate, load_sem.at[1])
    load_up = pltpu.make_async_copy(up_hbm.at[0, 0], up, load_sem.at[2])
    load_w = pltpu.make_async_copy(w_hbm.at[0], w, load_sem.at[3])
    load_go.start()

    right = lax.rem(me + 1, nz)
    left = lax.rem(me + nz - 1, nz)
    ahead = jnp.where(c == 0, right, left)
    barrier = pltpu.get_barrier_semaphore()
    for k in range(1, 8):
        pl.semaphore_signal(barrier, inc=1, device_id={"dp": lax.rem(dp + k, 8)}, device_id_type=MESH)
    for z in (left, right):
        pl.semaphore_signal(barrier, inc=1, device_id={"tensor": z}, device_id_type=MESH)
    load_gate.start()
    load_up.start()

    def place(core):
        even = 1 - lax.rem(y + 4 - core, 2)
        mate = lax.rem(y + 4 + 2 * even - 1, 4)
        outer = lax.rem(y + 4 - 2 * even + 1, 4)
        return 1 - even, mate, outer

    m_own, mate_own, outer_own = place(c)
    m_par, mate_par, _ = place(1 - c)
    q_own = 2 * m_own + c
    q_par = 2 * m_own + 1 - c
    base_own = lax.rem(y + 4 - m_own, 4)
    partner = 2 * y + 1 - c

    pad[...] = jnp.zeros_like(pad)
    load_go.wait()
    for u in range(2):
        pad[8 * u:8 * u + rows, :] = go[:, u * half:(u + 1) * half].astype(F32)
    first[...] = pad[...].astype(BF16)

    pl.semaphore_wait(barrier, 9)

    def first_copy(target_dp, q, k):
        return pltpu.make_async_remote_copy(
            src_ref=first, dst_ref=stage.at[q], send_sem=first_send.at[k], recv_sem=first_recv.at[q],
            device_id={"dp": target_dp}, device_id_type=MESH,
        )

    firsts = [
        first_copy(2 * mate_own + c, q_own, 0),
        first_copy(2 * mate_par + 1 - c, 2 * m_par + c, 1),
        first_copy(partner, 2 * m_par + c, 2),
    ]
    for one in firsts:
        one.start()
    stage[q_own] = first[...]

    load_gate.wait()
    load_up.wait()
    g32 = gate[...].astype(F32)
    u32 = up[...].astype(F32)
    logistic = 1.0 / (1.0 + jnp.exp(-g32))
    activated = g32 * logistic
    act[...] = activated
    gfac[...] = u32 * logistic * (1.0 + g32 * (1.0 - logistic))

    for k in (1, 2, 3):
        first_copy(partner, lax.rem(q_own + k, 4), 0).wait_recv()

    def pos(d):
        return lax.rem(d + top + c, top + 1)

    def at_slot(d):
        return pl.ds(pl.multiple_of(16 * pos(d), 16), 16)

    r = lax.broadcasted_iota(jnp.int32, (48, 64), 0)
    k = lax.broadcasted_iota(jnp.int32, (48, 64), 1)
    low = r % 16
    rho = jnp.where(r < 32, low, 16 + low % 8)
    u_of = jnp.where(r < 32, r // 16, low // 8)
    source = (rho // rows) * 16 + 8 * u_of + rho % rows
    pick = (source == k).astype(F32).astype(BF16)
    built = mm(pick, stage[...].reshape(64, half)).astype(BF16)
    for j in range(3):
        mine[j, at_slot(0), :] = built[16 * j:16 * j + 16, :]

    def z_copy(d, j, s):
        cols = pl.ds(s * width, width)
        return pltpu.make_async_remote_copy(
            src_ref=mine.at[j, at_slot(d), cols], dst_ref=mine.at[j, at_slot(d + 1), cols],
            send_sem=zs.at[lax.rem(d, 2), j, s], recv_sem=zr.at[d, j, s],
            device_id={"tensor": ahead}, device_id_type=MESH,
        )

    def y_copy(d):
        return pltpu.make_async_remote_copy(
            src_ref=mine.at[:, at_slot(d), :], dst_ref=other.at[:, at_slot(d), :],
            send_sem=ys.at[lax.rem(d, 2)], recv_sem=yr.at[pos(d)],
            device_id={"dp": 2 * outer_own + c}, device_id_type=MESH,
        )

    blocks = [(j, s) for j in range(3) for s in range(SPLITS)]
    for j, s in blocks:
        z_copy(0, j, s).start()

    @pl.when(c == 1)
    def _():
        y_copy(0).start()

    load_w.start()

    hidden_t[...] = jnp.transpose((act[...] * up[...].astype(F32)).astype(BF16).astype(F32)).astype(BF16)

    def h_copy(k, slot):
        to = lax.rem(y + k, 4)
        return pltpu.make_async_remote_copy(
            src_ref=hidden_t.at[pl.ds(pl.multiple_of(to * f2, 16), f2), :], dst_ref=h_in.at[c, slot],
            send_sem=hs.at[k], recv_sem=hr.at[slot],
            device_id={"dp": 2 * to + c}, device_id_type=MESH,
        )

    for k in (1, 2, 3):
        h_copy(k, y).start()
    h_in[c, y] = hidden_t[pl.ds(pl.multiple_of(y * f2, 16), f2), :]

    def step(d, carry, last=False):
        for j, s in blocks:
            z_copy(d - 1, j, s).wait_recv()
            if last:
                @pl.when(c == 0)
                def _():
                    z_copy(d, j, s).start()
            else:
                z_copy(d, j, s).start()

        @pl.when(d >= 3 - c)
        def _():
            y_copy(d).wait_send()

        y_copy(d).start()
        for j, s in blocks:
            z_copy(d - 1, j, s).wait_send()
        return carry

    def run(start, stop):
        lax.fori_loop(start, stop, step, 0)

    run(1, min(3, top - 1))

    for k in (1, 2, 3):
        h_copy(1, lax.rem(y + k, 4)).wait_recv()
    h_pass = pltpu.make_async_remote_copy(
        src_ref=h_in.at[c], dst_ref=h_in.at[c], send_sem=ps.at[0], recv_sem=pr.at[0],
        device_id={"dp": partner}, device_id_type=MESH,
    )
    h_pass.start()
    run(3, min(6, top - 1))

    def z_of(p, core):
        return lax.rem(jnp.where(core == 0, me + nz - 1 - p, me + p), nz)

    def select(count, q, kind, natural):
        t = lax.broadcasted_iota(jnp.int32, (count, ksize), 0)
        col = lax.broadcasted_iota(jnp.int32, (count, ksize), 1)
        low = col % 16
        p = col // 16
        start = (z_of(p, c) if natural else p) * rows
        if kind == 0:
            rho, valid = low, low >= 0
        else:
            rho, valid = 16 + low % 8, (low // 8) == (kind - 1)
        i = rho - rows * q
        hit = valid & (i >= 0) & (i < rows) & (t == start + i)
        return jnp.where(hit, 1.0, 0.0).astype(BF16)

    for kind in range(3):
        sel_g[kind, :tokens, :] = select(tokens, q_own, kind, True)
        sel_g[kind, tokens:, :] = select(part, q_par, kind, False)
    run(6, min(8, top - 1))
    h_pass.wait_recv()
    for group in range(2):
        base = lax.rem(base_own + 2 * group, 4)
        for kind in range(3):
            total = None
            for q in ((0, 1, 2) if kind == 0 else (2, 3)):
                h_q = h_in[q % 2, lax.rem(base + q // 2, 4)]
                term = mm(h_q, select(tokens, q, kind, True))
                total = term if total is None else total + term
            l_buf[group, kind] = total.astype(BF16)
    run(8, top - 1)
    step(top - 1, 0, last=True)

    @pl.when(c == 0)
    def _():
        for j, s in blocks:
            z_copy(top - 1, j, s).wait_recv()
        if top > 2:
            y_copy(top).wait_send()
        y_copy(top).start()

    tile = 256 if half % 256 == 0 else 128
    tiles = half // tile

    def tile_at(u, n):
        return pl.ds(pl.multiple_of(u * half + n * tile, tile), tile)

    for u in range(2):
        @pl.loop(0, tiles)
        def _(n):
            at = tile_at(0, n)
            got = mm(sel_g[0], mine[u, 0:ksize, at]) + mm(sel_g[1 + u], mine[2, 0:ksize, at])
            both = got.astype(BF16)
            g_buf[:, tile_at(u, n)] = both[:tokens]
            g_send[:, tile_at(u, n)] = both[tokens:]

    g_pass = pltpu.make_async_remote_copy(
        src_ref=g_send, dst_ref=g_recv, send_sem=ps.at[1], recv_sem=pr.at[1],
        device_id={"dp": partner}, device_id_type=MESH,
    )
    g_pass.start()

    before = jnp.int32(0)
    for k in range(npipe):
        before = before + jnp.where(section >= k, layers_ref[k], 0)
    scale = jnp.sqrt(10.0 / jnp.full((1, 128), before, jnp.int32).astype(F32))[:, :1]
    norm_scale = scale / jnp.sqrt(jnp.full((1, 1), tokens * 8, F32))

    for p in range(top):
        pltpu.make_async_remote_copy(
            src_ref=mine.at[:, 0:16, :], dst_ref=other.at[:, 16 * p:16 * p + 16, :],
            send_sem=ys.at[0], recv_sem=yr.at[p],
            device_id={"dp": 2 * outer_own + c}, device_id_type=MESH,
        ).wait_recv()

    for u in range(2):
        @pl.loop(0, tiles)
        def _(n):
            at = tile_at(0, n)
            total = mm(l_buf[0, 0], mine[u, 0:ksize, at]) + mm(l_buf[0, 1 + u], mine[2, 0:ksize, at])
            total = total + mm(l_buf[1, 0], other[u, 0:ksize, at]) + mm(l_buf[1, 1 + u], other[2, 0:ksize, at])
            total = total * norm_scale
            low_rows, high_rows = total[:fb], total[fb:]
            d_own[:, tile_at(u, n)] = jnp.where(c == 0, low_rows, high_rows)
            d_send[:, tile_at(u, n)] = jnp.where(c == 0, high_rows, low_rows).astype(BF16)

    d_pass = pltpu.make_async_remote_copy(
        src_ref=d_send, dst_ref=d_recv, send_sem=ps.at[2], recv_sem=pr.at[2],
        device_id={"dp": partner}, device_id_type=MESH,
    )
    d_pass.start()

    t = lax.broadcasted_iota(jnp.int32, (tokens, part), 0)
    col = lax.broadcasted_iota(jnp.int32, (tokens, part), 1)
    spread = jnp.where(t == z_of(col // rows, 1 - c) * rows + col % rows, 1.0, 0.0).astype(BF16)
    g_pass.wait_recv()

    @pl.loop(0, 2 * tiles)
    def _(n):
        at = tile_at(0, n)
        g_buf[:, at] = (g_buf[:, at].astype(F32) + mm(spread, g_recv[:, at])).astype(BF16)

    load_w.wait()
    at = 0
    while at < ff:
        n = min(256, ff - at)
        gh = scale * lax.dot_general(
            g_buf[...], w[at:at + n, :], (((1,), (1,)), ((), ())), preferred_element_type=F32)
        gg_ref[0, 0, :, at:at + n] = (gh * gfac[:, at:at + n]).astype(BF16)
        gu_ref[0, 0, :, at:at + n] = (gh * act[:, at:at + n]).astype(BF16)
        at += n

    d_pass.wait()

    @pl.loop(0, 2 * tiles)
    def _(n):
        at = tile_at(0, n)
        dw_ref[0, :, at] = (d_own[:, at] + d_recv[:, at].astype(F32)).astype(BF16)

    y_copy(0).wait_send()
    y_copy(1).wait_send()

    @pl.when(c == 0)
    def _():
        for j, s in blocks:
            z_copy(top - 1, j, s).wait_send()

    for one in firsts:
        one.wait_send()
    for k in (1, 2, 3):
        h_copy(k, y).wait_send()
    h_pass.wait_send()
    g_pass.wait_send()


def put_out(gg_ref, gu_ref, dw_ref, gg_hbm, gu_hbm, dw_hbm, sem):
    copies = [
        pltpu.make_async_copy(gg_ref, gg_hbm, sem.at[0]),
        pltpu.make_async_copy(gu_ref, gu_hbm, sem.at[1]),
        pltpu.make_async_copy(dw_ref, dw_hbm, sem.at[2]),
    ]
    for one in copies:
        one.start()
    for one in copies:
        one.wait()


def per_device(section_layers, grad_out, gate_act, up_act, down_weight, *, sizes):
    npipe, nz = sizes
    rows, d = grad_out.shape[2:]
    tokens, ff = gate_act.shape[2:]
    fb = ff // 8
    top = nz // 2
    ksize = 16 * top
    part = rows * top
    any_spec = pl.BlockSpec(memory_space=pltpu.HBM)
    vmem_spec = pl.BlockSpec(memory_space=pltpu.VMEM)
    outs = (
        jax.ShapeDtypeStruct(gate_act.shape, BF16),
        jax.ShapeDtypeStruct(gate_act.shape, BF16),
        jax.ShapeDtypeStruct((1, fb, d), BF16),
    )
    section_layers, grad_out, gate_act, up_act, down_weight = (
        pltpu.with_memory_space_constraint(x, pltpu.HBM) for x in (section_layers, grad_out, gate_act, up_act, down_weight))
    got = pl.pallas_call(
        functools.partial(kernel, nz, npipe),
        out_shape=outs,
        in_specs=[pl.BlockSpec(memory_space=pltpu.SMEM)] + [any_spec] * 4,
        out_specs=(vmem_spec,) * 3,
        scratch_shapes=[
            pltpu.VMEM((rows, d), BF16),
            pltpu.VMEM((tokens, ff), BF16),
            pltpu.VMEM((tokens, ff), BF16),
            pltpu.VMEM((ff, d), BF16),
            pltpu.VMEM((16, d // 2), F32),
            pltpu.VMEM((16, d // 2), BF16),
            pltpu.VMEM((4, 16, d // 2), BF16),
            pltpu.VMEM((3, ksize + 16, d // 2), BF16),
            pltpu.VMEM((3, ksize + 16, d // 2), BF16),
            pltpu.VMEM((tokens, ff), F32),
            pltpu.VMEM((tokens, ff), F32),
            pltpu.VMEM((ff, tokens), BF16),
            pltpu.VMEM((2, 4, 2 * fb, tokens), BF16),
            pltpu.VMEM((2, 3, 2 * fb, ksize), BF16),
            pltpu.VMEM((3, tokens + part, ksize), BF16),
            pltpu.VMEM((part, d), BF16),
            pltpu.VMEM((part, d), BF16),
            pltpu.VMEM((tokens, d), BF16),
            pltpu.VMEM((fb, d), BF16),
            pltpu.VMEM((fb, d), BF16),
            pltpu.VMEM((fb, d), F32),
            pltpu.SemaphoreType.DMA((4,)),
            pltpu.SemaphoreType.DMA((3,)),
            pltpu.SemaphoreType.DMA((4,)),
            pltpu.SemaphoreType.DMA((2, 3, SPLITS)),
            pltpu.SemaphoreType.DMA((top, 3, SPLITS)),
            pltpu.SemaphoreType.DMA((2,)),
            pltpu.SemaphoreType.DMA((top,)),
            pltpu.SemaphoreType.DMA((4,)),
            pltpu.SemaphoreType.DMA((4,)),
            pltpu.SemaphoreType.DMA((3,)),
            pltpu.SemaphoreType.DMA((3,)),
        ],
        compiler_params=pltpu.CompilerParams(
            collective_id=0, has_side_effects=True, vmem_limit_bytes=44 * 2**20
        ),
    )(section_layers, grad_out, gate_act, up_act, down_weight)
    return pl.pallas_call(
        put_out,
        out_shape=outs,
        in_specs=[vmem_spec] * 3,
        out_specs=(any_spec,) * 3,
        scratch_shapes=[pltpu.SemaphoreType.DMA((3,))],
        compiler_params=pltpu.CompilerParams(vmem_limit_bytes=8 * 2**20),
    )(*got)


def solution(mesh):
    placed = (
        P(),
        P("pipe", "dp", "tensor", None),
        P("pipe", "dp", None, "tensor"),
        P("pipe", "dp", None, "tensor"),
        P("pipe", "tensor", None),
    )
    return jax.shard_map(
        functools.partial(per_device, sizes=(mesh.shape["pipe"], mesh.shape["tensor"])),
        mesh=mesh,
        in_specs=placed,
        out_specs=(
            P("pipe", "dp", None, "tensor"),
            P("pipe", "dp", None, "tensor"),
            P("pipe", ("tensor", "dp"), None),
        ),
        check_vma=False,
    )
```
